512 devices in a mesh: rows: 32 (over x_hi, y, core), snaps: 16 (over z, x_lo).
Axes of the slice: x: 4 (x_hi: 2, x_lo: 2; x = x_hi * 2 + x_lo), y: 8, z: 8, core: 2. Of those that a mesh axis runs over, the one named last changes fastest.
Arguments:
- snapshots: bfloat16 [4096, 32768], P('rows', 'snaps'), may hold values from -6 to 6
- linear_basis: bfloat16 [4096, 64], P(('rows', 'snaps')), may hold values from -0.75 to 0.75
- quad_weights: bfloat16 [4096, 2080], P(('rows', 'snaps')), may hold values from -0.125 to 0.125
- coordinates: bfloat16 [64, 32768], P(None, 'snaps'), may hold values from -5 to 5
Outputs:
- grad_basis: float32 [4096, 64], P(('rows', 'snaps'))
- grad_quad: float32 [4096, 2080], P(('rows', 'snaps'))
- grad_coords: float32 [64, 32768], P('rows', 'snaps')
The draws below stay inside these ranges and needn't reach their ends.
All inputs are finite; a program needn't handle non-finite values.
Results may differ from the reference program's by a relative error of at most 0.0012.
Values may be sent and summed in bfloat16 or wider, within the bound.
No kernel may reach another device: no remote copies, remote signals or barrier semaphores. Data moves between devices by JAX's collectives and lax.ppermute only.
A program may use at most 64 MiB of HBM per device.

```python
import jax
import jax.numpy as jnp
from jax import lax

R = 64
F = 2080
SNAP_DEV = 2048
ROWS = 4096
SNAPS = 32768


def levels(own_key, extent, split, least, high):
    def one(position, blocks):
        steps = jax.random.uniform(jax.random.fold_in(jax.random.fold_in(own_key, 6), position), (blocks,), jnp.float32, least / len(split), high / len(split))
        return jnp.repeat(jnp.exp(steps), extent[position] // blocks).reshape((-1,) + (1,) * (len(extent) - position - 1))

    loudness = one(*split[0])
    for cut in split[1:]:
        loudness = loudness * one(*cut)
    return loudness


def centred(stream_key, dims, scale, bound, shards=(), held_as=jnp.bfloat16):
    values = jax.random.normal(stream_key, dims, jnp.float32) * scale
    if len(shards) > 0:
        values = levels(stream_key, dims, shards, -0.22, 0.18) * values
    return jnp.clip(values, min=-bound, max=bound).astype(held_as)


def setup_inputs(seed: int = 0) -> dict:
    splits = jax.random.split(jax.random.key(seed), 5)
    return {
        "snapshots": centred(splits[0], (ROWS, SNAPS), 1.0, 6.0, ((0, 32), (1, 16))),
        "linear_basis": centred(splits[1], (ROWS, R), R ** -0.5, 0.75, ((0, 512),)),
        "quad_weights": centred(splits[2], (ROWS, F), F ** -0.5, 0.125, ((0, 512),)),
        "coordinates": centred(splits[3], (R, SNAPS), 1.0, 5.0, ((1, 16),)),
    }


def quad_feats(coord_vals):
    count = coord_vals.shape[0]
    return jnp.concatenate([coord_vals[lead:lead + 1] * coord_vals[lead:] for lead in range(count)], axis=0).astype(jnp.bfloat16)

def chain_rule(back_quad, coord_vals):
    count = coord_vals.shape[0]
    result = jnp.zeros_like(coord_vals)
    offset = 0
    for lead in range(count):
        block_rows = back_quad[offset:offset + count - lead]
        result = result.at[lead].add(lax.optimization_barrier(jnp.sum(block_rows * coord_vals[lead:], axis=0)))
        result = result.at[lead:].add(block_rows * coord_vals[lead])
        offset += count - lead
    return result

def reference(snapshots, linear_basis, quad_weights, coordinates):
    maps = jnp.concatenate([linear_basis, quad_weights], axis=1).astype(jnp.float32)
    block_count = SNAPS // SNAP_DEV
    snap_blocks = snapshots.reshape(ROWS, block_count, SNAP_DEV).transpose(1, 0, 2)
    coord_blocks = coordinates.reshape(R, block_count, SNAP_DEV).transpose(1, 0, 2)
    high = lax.Precision.HIGHEST

    def block_step(model_grad, block_pair):
        coord_vals = block_pair[1].astype(jnp.float32)
        quad = lax.optimization_barrier(quad_feats(coord_vals))
        features = jnp.concatenate([block_pair[1], quad], axis=0).astype(jnp.float32)
        rebuilt = jnp.dot(maps, features, precision=high)
        residual = lax.optimization_barrier((rebuilt - block_pair[0].astype(jnp.float32)).astype(jnp.bfloat16))
        residual = residual.astype(jnp.float32)
        model_grad = model_grad + jnp.dot(residual, features.T, precision=high)
        back = jnp.dot(maps.T, residual, precision=high)
        coord_part = back[:R] + chain_rule(back[R:], coord_vals)
        return (model_grad, coord_part)
    start_grad = jnp.zeros((ROWS, R + F), jnp.float32)
    model_grad, coord_parts = lax.scan(block_step, start_grad, (snap_blocks, coord_blocks))
    model_grad = model_grad / jnp.sqrt(jnp.float32(SNAPS))
    grad_coords = coord_parts.transpose(1, 0, 2).reshape(R, SNAPS) / jnp.sqrt(jnp.float32(ROWS))
    return (model_grad[:, :R], model_grad[:, R:], grad_coords)
```

```python
import math

import jax
import jax.numpy as jnp
import numpy as np
from jax import lax
from jax.sharding import PartitionSpec as P


def pair_tables(count):
    lead_index, tail_index = np.triu_indices(count)
    pair_total = lead_index.shape[0]
    lead_table = np.zeros((pair_total, count), np.float32)
    tail_table = np.zeros((pair_total, count), np.float32)
    lead_table[np.arange(pair_total), lead_index] = 1.0
    tail_table[np.arange(pair_total), tail_index] = 1.0
    return (lead_table, tail_table)


def shards(snapshots, linear_basis, quad_weights, coordinates):
    coord_count = coordinates.shape[0]
    local_rows, snap_dev = snapshots.shape
    high = lax.Precision.HIGHEST
    lead_np, tail_np = pair_tables(coord_count)
    lead_f32 = jnp.asarray(lead_np)
    tail_f32 = jnp.asarray(tail_np)
    lead_bf16 = lead_f32.astype(jnp.bfloat16)
    tail_bf16 = tail_f32.astype(jnp.bfloat16)
    snap_parts = lax.axis_size("snaps")
    row_parts = lax.axis_size("rows")
    own_maps = jnp.concatenate([linear_basis, quad_weights], axis=1)
    own_maps = jnp.broadcast_to(own_maps[None], (snap_parts,) + own_maps.shape)
    maps = lax.all_to_all(own_maps, "snaps", 0, 0, tiled=True).reshape(local_rows, -1)
    lin_rows, quad_rows = maps[:, :coord_count], maps[:, coord_count:]
    block_width = min(256, snap_dev)
    block_total = snap_dev // block_width
    contract_rows = (((0,), (0,)), ((), ()))
    contract_cols = (((1,), (1,)), ((), ()))

    def block_core(start_col):
        coord_block = lax.dynamic_slice_in_dim(coordinates, start_col, block_width, 1)
        snap_block = lax.dynamic_slice_in_dim(snapshots, start_col, block_width, 1)
        lead_vals = jnp.dot(lead_bf16, coord_block, preferred_element_type=jnp.float32)
        tail_vals = jnp.dot(tail_bf16, coord_block, preferred_element_type=jnp.float32)
        quad_block = (lead_vals * tail_vals).astype(jnp.bfloat16)
        rebuilt = jnp.dot(lin_rows, coord_block, preferred_element_type=jnp.float32)
        rebuilt = rebuilt + jnp.dot(quad_rows, quad_block, preferred_element_type=jnp.float32)
        residual = (rebuilt - snap_block.astype(jnp.float32)).astype(jnp.bfloat16)
        back_lin = lax.dot_general(
            lin_rows, residual, contract_rows, preferred_element_type=jnp.float32
        )
        back_quad = lax.dot_general(
            quad_rows, residual, contract_rows, preferred_element_type=jnp.float32
        )
        terms = back_lin + lax.dot_general(
            lead_f32, back_quad * tail_vals, contract_rows, precision=high
        )
        terms = terms + lax.dot_general(
            tail_f32, back_quad * lead_vals, contract_rows, precision=high
        )
        return (coord_block, quad_block, residual, terms)

    def block_step(block_index, loop_state):
        lin_grad, quad_grad, coord_part = loop_state
        start_col = block_index * block_width
        coord_block, quad_block, residual, terms = block_core(start_col)
        lin_grad = lin_grad + lax.dot_general(
            residual, coord_block, contract_cols, preferred_element_type=jnp.float32
        )
        quad_grad = quad_grad + lax.dot_general(
            residual, quad_block, contract_cols, preferred_element_type=jnp.float32
        )
        coord_part = lax.dynamic_update_slice_in_dim(coord_part, terms, start_col, 1)
        return (lin_grad, quad_grad, coord_part)

    start_state = (
        jnp.zeros((local_rows, coord_count), jnp.float32),
        jnp.zeros((local_rows, quad_weights.shape[1]), jnp.float32),
        jnp.zeros((coord_count, snap_dev), jnp.float32),
    )
    lin_grad, quad_grad, coord_part = lax.fori_loop(0, block_total, block_step, start_state)
    model_grad = jnp.concatenate([lin_grad, quad_grad], axis=1)
    model_grad = model_grad.reshape(snap_parts, -1, model_grad.shape[1])
    model_sum = jnp.sum(lax.all_to_all(model_grad, "snaps", 0, 0, tiled=True), axis=0)
    lin_sum, quad_sum = model_sum[:, :coord_count], model_sum[:, coord_count:]
    coord_part = coord_part.reshape(row_parts, -1, snap_dev)
    coord_share = jnp.sum(lax.all_to_all(coord_part, "rows", 0, 0, tiled=True), axis=0)
    grad_coords = coord_share * (1.0 / math.sqrt(local_rows * row_parts))
    model_scale = 1.0 / math.sqrt(snap_dev * lax.axis_size("snaps"))
    return (lin_sum * model_scale, quad_sum * model_scale, grad_coords)


def solution(mesh):
    placed = (
        P("rows", "snaps"),
        P(("rows", "snaps"), None),
        P(("rows", "snaps"), None),
        P(None, "snaps"),
    )
    return jax.shard_map(
        shards,
        mesh=mesh,
        in_specs=placed,
        out_specs=(P(("rows", "snaps"), None), P(("rows", "snaps"), None), P("rows", "snaps")),
        check_vma=False,
    )
```

```python
import math

import jax
import jax.numpy as jnp
import numpy as np
from jax import lax
from jax.experimental import pallas as pl
from jax.experimental.pallas import tpu as pltpu
from jax.sharding import PartitionSpec as P


LANES = 128
BLOCK = 256
WIDE = 512
TOP = 14.0
CORES, FAR, RING = 2, 2, 8


def coordinate_order(count):
    each = count // (CORES * FAR * RING)
    return np.arange(count).reshape(FAR, RING, CORES, each).transpose(2, 0, 1, 3).reshape(-1)


def column_source(count):
    order = coordinate_order(count)
    offset = np.cumsum([0] + [count - i for i in range(count)])
    source = []
    for d in range(count // 2 + 1):
        for k in range(count):
            i, j = sorted((order[k], order[(k + d) % count]))
            source.append(-1 if d == count // 2 and k >= d else offset[i] + j - i)
    return np.concatenate([source, offset[-1] + order])


def gather_tables(source):
    pad = -len(source) % LANES
    source = np.concatenate([source, np.full(pad, -1)]).reshape(-1, 1, LANES)
    source = np.broadcast_to(source, (source.shape[0], 8, LANES)).astype(np.int32)
    return np.where(source < 0, 0, source % LANES), np.where(source < 0, -1, source // LANES)


def permuted(tiles, lane, tile):
    total = jnp.zeros(tiles[0].shape, jnp.float32)
    for number, values in enumerate(tiles):
        moved = jnp.take_along_axis(values, lane, axis=1)
        total = jnp.where(tile == number, moved, total)
    return total


def tiles_of(values):
    return [values[:, t : t + LANES] for t in range(0, values.shape[1], LANES)]


def spread_kernel(lin_ref, quad_ref, lane_ref, tile_ref, out_ref, wide_ref):
    pairs = quad_ref.shape[1]
    wide_ref[...] = jnp.zeros_like(wide_ref)
    wide_ref[:, :pairs] = quad_ref[...].astype(jnp.float32)
    wide_ref[:, pairs : pairs + lin_ref.shape[1]] = lin_ref[...].astype(jnp.float32)
    tiles = tiles_of(wide_ref[...])
    for t in range(lane_ref.shape[0]):
        moved = permuted(tiles, lane_ref[t], tile_ref[t]).astype(jnp.bfloat16)
        for c in range(out_ref.shape[0]):
            out_ref[c, :, t * LANES : (t + 1) * LANES] = moved


def turned(values, count, step):
    step %= count
    return values if step == 0 else jnp.concatenate([values[step:], values[:step]], axis=0)


def forward_kernel(pairs, maps_ref, coord_ref, snap_ref, grad_ref, res_ref, feat_ref):
    count, columns = coord_ref.shape
    rows, width = maps_ref.shape
    blocks = [slice(n, n + WIDE) for n in range(0, columns, WIDE)]

    def features(block):
        for start in range(block.start, block.stop, LANES):
            part = slice(start, start + LANES)
            coord = coord_ref[:, part].astype(jnp.float32)
            for r in range(8):
                shifted = coord if r == 0 else pltpu.roll(coord, count - r, 0)
                for d in range(r, count // 2 + 1, 8):
                    feat_ref[d * count : (d + 1) * count, part] = (
                        coord * turned(shifted, count, d - r)
                    ).astype(jnp.bfloat16)
            feat_ref[width - count :, part] = coord_ref[:, part]

    features(blocks[0])
    for n, block in enumerate(blocks):
        rebuilt = jnp.dot(maps_ref[...], feat_ref[:, block], preferred_element_type=jnp.float32)
        if n + 1 < len(blocks):
            features(blocks[n + 1])
        res_ref[:, block] = (rebuilt - snap_ref[:, block].astype(jnp.float32)).astype(jnp.bfloat16)
    top = jnp.zeros((rows, LANES), jnp.float32)
    for start in range(0, width, WIDE):
        part = slice(start, min(start + WIDE, width))
        grad = lax.dot_general(
            res_ref[...], feat_ref[part], (((1,), (1,)), ((), ())), preferred_element_type=jnp.float32
        )
        grad_ref[:, part] = grad
        for tile in tiles_of(grad):
            top = jnp.maximum(top, jnp.abs(tile))
    top = jnp.max(jnp.max(top, axis=0, keepdims=True), axis=1, keepdims=True)
    level = jnp.floor(jnp.log2(jnp.maximum(top, 2.0**-100)))
    scale = jnp.exp2(TOP - level)
    for start in range(0, width, LANES):
        part = slice(start, start + LANES)
        values = grad_ref[:, part] * scale
        if start <= pairs < start + LANES:
            lane = lax.broadcasted_iota(jnp.int32, values.shape, 1) + start
            values = jnp.where((lane >= pairs) & (lane < width - count), level, values)
        grad_ref[:, part] = values


def backward_kernel(scale, maps_ref, coord_ref, res_ref, out_ref, turn_ref):
    count = coord_ref.shape[0]
    width = maps_ref.shape[1]

    @pl.when(pl.program_id(0) == 0)
    def _():
        turn_ref[...] = maps_ref[...].astype(jnp.float32).T.astype(jnp.bfloat16)

    coord = coord_ref[...].astype(jnp.float32)
    residual = res_ref[...]

    def back(row):
        return jnp.dot(turn_ref[row : row + count], residual, preferred_element_type=jnp.float32)

    total = back(width - count)
    for r in range(8):
        shifted = coord if r == 0 else pltpu.roll(coord, count - r, 0)
        spun = jnp.zeros_like(coord)
        for d in range(r, count // 2 + 1, 8):
            part = back(d * count)
            total = total + part * turned(shifted, count, d - r)
            spun = spun + turned(part * coord, count, r - d)
        total = total + (spun if r == 0 else pltpu.roll(spun, r, 0))
    out_ref[...] = total * scale


def gather_kernel(scale, parts_ref, lane_ref, tile_ref, lin_ref, quad_ref, wide_ref):
    pairs = quad_ref.shape[1]
    total = jnp.zeros(parts_ref.shape[1:], jnp.float32)
    for p in range(parts_ref.shape[0]):
        part = parts_ref[p]
        total = total + part * jnp.exp2(part[:, pairs : pairs + 1] - TOP)
    tiles = tiles_of(total * scale)
    for t in range(lane_ref.shape[0]):
        wide_ref[:, t * LANES : (t + 1) * LANES] = permuted(tiles, lane_ref[t], tile_ref[t])
    quad_ref[...] = wide_ref[:, :pairs]
    lin_ref[...] = wide_ref[:, pairs : pairs + lin_ref.shape[1]]


def shards(snapshots, linear_basis, quad_weights, coordinates):
    count = coordinates.shape[0]
    local_rows, snap_dev = snapshots.shape
    own_rows, pairs = quad_weights.shape
    snap_parts = lax.axis_size("snaps")
    row_parts = lax.axis_size("rows")
    assert row_parts == CORES * FAR * RING and (pairs + count) % 32 == 0
    source = column_source(count)
    width = len(source)
    padded = pairs + count + -(pairs + count) % LANES
    lane, tile = gather_tables(source)
    back_source = np.zeros(pairs + count, np.int64)
    back_source[source[source >= 0]] = np.nonzero(source >= 0)[0]
    back_lane, back_tile = gather_tables(back_source)

    own = pl.pallas_call(
        spread_kernel,
        out_shape=jax.ShapeDtypeStruct((snap_parts, own_rows, width), jnp.bfloat16),
        scratch_shapes=[pltpu.VMEM((own_rows, padded), jnp.float32)],
    )(linear_basis, quad_weights, jnp.asarray(lane), jnp.asarray(tile))
    maps = lax.all_to_all(own, "snaps", 0, 0, tiled=True).reshape(local_rows, width)
    coords = coordinates.reshape(FAR, RING, CORES, -1, snap_dev).transpose(2, 0, 1, 3, 4).reshape(count, snap_dev)

    flops = 2 * local_rows * width * snap_dev
    grad, residual = pl.pallas_call(
        lambda *refs: forward_kernel(pairs, *refs),
        out_shape=[
            jax.ShapeDtypeStruct((local_rows, width), jnp.float32),
            jax.ShapeDtypeStruct((local_rows, snap_dev), jnp.bfloat16),
        ],
        scratch_shapes=[pltpu.VMEM((width, snap_dev), jnp.bfloat16)],
        compiler_params=pltpu.CompilerParams(vmem_limit_bytes=24 << 20),
        cost_estimate=pl.CostEstimate(flops=2 * flops, bytes_accessed=4 << 20, transcendentals=0),
    )(maps, coords, snapshots)
    grad = grad.astype(jnp.float16).reshape(snap_parts, own_rows, width)
    grad_parts = lax.all_to_all(grad, "snaps", 0, 0, tiled=True)

    block = min(BLOCK, snap_dev)
    coord_scale = 1.0 / math.sqrt(local_rows * row_parts)
    coord_part = pl.pallas_call(
        lambda *refs: backward_kernel(coord_scale, *refs),
        grid=(snap_dev // block,),
        in_specs=[
            pl.BlockSpec((local_rows, width), lambda n: (0, 0), pipeline_mode=pl.Buffered(1)),
            pl.BlockSpec((count, block), lambda n: (0, n)),
            pl.BlockSpec((local_rows, block), lambda n: (0, n)),
        ],
        out_specs=pl.BlockSpec((count, block), lambda n: (0, n)),
        out_shape=jax.ShapeDtypeStruct((count, snap_dev), jnp.float32),
        scratch_shapes=[pltpu.VMEM((width, local_rows), jnp.bfloat16)],
        compiler_params=pltpu.CompilerParams(vmem_limit_bytes=24 << 20),
        cost_estimate=pl.CostEstimate(flops=flops, bytes_accessed=2 << 20, transcendentals=0),
    )(maps, coords, residual)

    place = lax.axis_index("rows")
    for apart, own_half in ((1, place % CORES), (CORES * RING, place // (CORES * RING))):
        half = coord_part.shape[0] // 2
        sent = lax.dynamic_slice_in_dim(coord_part, (1 - own_half) * half, half, 0)
        kept = lax.dynamic_slice_in_dim(coord_part, own_half * half, half, 0)
        came = lax.ppermute(sent, "rows", [(i, i ^ apart) for i in range(row_parts)])
        coord_part = kept + came
    rings = [[(f * RING + y) * CORES + c for y in range(RING)] for f in range(FAR) for c in range(CORES)]
    coord_parts = lax.all_to_all(
        coord_part.reshape(RING, -1, snap_dev), "rows", 0, 0, axis_index_groups=rings, tiled=True
    )
    grad_coords = jnp.sum(coord_parts, axis=0)

    model_scale = 1.0 / math.sqrt(snap_dev * snap_parts)
    grad_basis, grad_quad = pl.pallas_call(
        lambda *refs: gather_kernel(model_scale, *refs),
        out_shape=[
            jax.ShapeDtypeStruct(linear_basis.shape, jnp.float32),
            jax.ShapeDtypeStruct(quad_weights.shape, jnp.float32),
        ],
        scratch_shapes=[pltpu.VMEM((own_rows, padded), jnp.float32)],
    )(grad_parts.astype(jnp.float32), jnp.asarray(back_lane), jnp.asarray(back_tile))
    return (grad_basis, grad_quad, grad_coords)


def solution(mesh):
    placed = (
        P("rows", "snaps"),
        P(("rows", "snaps"), None),
        P(("rows", "snaps"), None),
        P(None, "snaps"),
    )

    return jax.shard_map(
        shards,
        mesh=mesh,
        in_specs=placed,
        out_specs=(P(("rows", "snaps"), None), P(("rows", "snaps"), None), P("rows", "snaps")),
        check_vma=False,
    )
```

```python
import math

import jax
import jax.numpy as jnp
import numpy as np
from jax import lax
from jax.experimental import pallas as pl
from jax.experimental.pallas import tpu as pltpu
from jax.sharding import PartitionSpec as P


LANES = 128
BLOCK = 256
WIDE = 512
TOP = 14.0
CORES, FAR, RING = 2, 2, 8


def coordinate_order(count):
    each = count // (CORES * FAR * RING)
    return np.arange(count).reshape(FAR, RING, CORES, each).transpose(2, 0, 1, 3).reshape(-1)


def column_source(count):
    order = coordinate_order(count)
    offset = np.cumsum([0] + [count - i for i in range(count)])
    source = []
    for d in range(count // 2 + 1):
        for k in range(count):
            i, j = sorted((order[k], order[(k + d) % count]))
            source.append(-1 if d == count // 2 and k >= d else offset[i] + j - i)
    return np.concatenate([source, offset[-1] + order])


def gather_table(source):
    return jnp.asarray(np.concatenate([source, np.full(-len(source) % LANES, -1)]).reshape(-1, LANES).astype(np.int32))


def permuted(tiles, table_ref, row):
    source = jnp.broadcast_to(table_ref[row : row + 1], tiles[0].shape)
    lane, tile = source & (LANES - 1), source >> 7
    total = jnp.zeros(tiles[0].shape, jnp.float32)
    for number, values in enumerate(tiles):
        total = jnp.where(tile == number, jnp.take_along_axis(values, lane, axis=1), total)
    return total


def tiles_of(values):
    return [values[:, t : t + LANES] for t in range(0, values.shape[1], LANES)]


def spread_kernel(lin_ref, quad_ref, table_ref, out_ref, wide_ref):
    pairs = quad_ref.shape[1]
    wide_ref[...] = jnp.zeros_like(wide_ref)
    wide_ref[:, :pairs] = quad_ref[...].astype(jnp.float32)
    wide_ref[:, pairs : pairs + lin_ref.shape[1]] = lin_ref[...].astype(jnp.float32)
    tiles = tiles_of(wide_ref[...])
    for t in range(table_ref.shape[0]):
        moved = permuted(tiles, table_ref, t).astype(jnp.bfloat16)
        for c in range(out_ref.shape[0]):
            out_ref[c, :, t * LANES : (t + 1) * LANES] = moved


def turned(values, count, step):
    step %= count
    return values if step == 0 else jnp.concatenate([values[step:], values[:step]], axis=0)


def forward_kernel(pairs, maps_ref, coord_ref, snap_ref, grad_ref, res_ref, feat_ref):
    count, columns = coord_ref.shape
    rows, width = maps_ref.shape
    blocks = [slice(n, n + WIDE) for n in range(0, columns, WIDE)]

    def features(block):
        for start in range(block.start, block.stop, LANES):
            part = slice(start, start + LANES)
            coord = coord_ref[:, part].astype(jnp.float32)
            for r in range(8):
                shifted = coord if r == 0 else pltpu.roll(coord, count - r, 0)
                for d in range(r, count // 2 + 1, 8):
                    feat_ref[d * count : (d + 1) * count, part] = (
                        coord * turned(shifted, count, d - r)
                    ).astype(jnp.bfloat16)
            feat_ref[width - count :, part] = coord_ref[:, part]

    features(blocks[0])
    for n, block in enumerate(blocks):
        rebuilt = jnp.dot(maps_ref[...], feat_ref[:, block], preferred_element_type=jnp.float32)
        if n + 1 < len(blocks):
            features(blocks[n + 1])
        res_ref[:, block] = (rebuilt - snap_ref[:, block].astype(jnp.float32)).astype(jnp.bfloat16)
    top = jnp.zeros((rows, LANES), jnp.float32)
    for start in range(0, width, WIDE):
        part = slice(start, min(start + WIDE, width))
        grad = lax.dot_general(
            res_ref[...], feat_ref[part], (((1,), (1,)), ((), ())), preferred_element_type=jnp.float32
        )
        grad_ref[:, part] = grad
        for tile in tiles_of(grad):
            top = jnp.maximum(top, jnp.abs(tile))
    top = jnp.max(jnp.max(top, axis=0, keepdims=True), axis=1, keepdims=True)
    level = jnp.floor(jnp.log2(jnp.maximum(top, 2.0**-100)))
    scale = jnp.exp2(TOP - level)
    for start in range(0, width, LANES):
        part = slice(start, start + LANES)
        values = grad_ref[:, part] * scale
        if start <= pairs < start + LANES:
            lane = lax.broadcasted_iota(jnp.int32, values.shape, 1) + start
            values = jnp.where((lane >= pairs) & (lane < width - count), level, values)
        grad_ref[:, part] = values


def backward_kernel(scale, maps_ref, coord_ref, res_ref, out_ref, turn_ref):
    count = coord_ref.shape[0]
    width = maps_ref.shape[1]

    @pl.when(pl.program_id(0) == 0)
    def _():
        turn_ref[...] = maps_ref[...].astype(jnp.float32).T.astype(jnp.bfloat16)

    coord = coord_ref[...].astype(jnp.float32)
    residual = res_ref[...]

    def back(row):
        return jnp.dot(turn_ref[row : row + count], residual, preferred_element_type=jnp.float32)

    total = back(width - count)
    for r in range(8):
        shifted = coord if r == 0 else pltpu.roll(coord, count - r, 0)
        spun = jnp.zeros_like(coord)
        for d in range(r, count // 2 + 1, 8):
            part = back(d * count)
            total = total + part * turned(shifted, count, d - r)
            spun = spun + turned(part * coord, count, r - d)
        total = total + (spun if r == 0 else pltpu.roll(spun, r, 0))
    out_ref[...] = total * scale


def pack_kernel(kept_ref, came_ref, out_ref):
    columns = kept_ref.shape[1]
    total = kept_ref[...] + came_ref[...]
    top = jnp.max(jnp.max(jnp.abs(total), axis=0, keepdims=True), axis=1, keepdims=True)
    level = jnp.floor(jnp.log2(jnp.maximum(top, 2.0**-100)))
    out_ref[:, :columns] = total * jnp.exp2(TOP - level)
    out_ref[:, columns:] = jnp.broadcast_to(level, (total.shape[0], LANES))


def unpack_kernel(parts_ref, out_ref):
    columns = out_ref.shape[1]
    total = jnp.zeros(out_ref.shape, jnp.float32)
    for p in range(parts_ref.shape[0]):
        part = parts_ref[p]
        total = total + part[:, :columns] * jnp.exp2(part[:, columns : columns + 1] - TOP)
    out_ref[...] = total


def gather_kernel(scale, parts_ref, table_ref, lin_ref, quad_ref, wide_ref):
    pairs = quad_ref.shape[1]
    total = jnp.zeros(parts_ref.shape[1:], jnp.float32)
    for p in range(parts_ref.shape[0]):
        part = parts_ref[p]
        total = total + part * jnp.exp2(part[:, pairs : pairs + 1] - TOP)
    tiles = tiles_of(total * scale)
    for t in range(table_ref.shape[0]):
        wide_ref[:, t * LANES : (t + 1) * LANES] = permuted(tiles, table_ref, t)
    quad_ref[...] = wide_ref[:, :pairs]
    lin_ref[...] = wide_ref[:, pairs : pairs + lin_ref.shape[1]]


def shards(snapshots, linear_basis, quad_weights, coordinates):
    count = coordinates.shape[0]
    local_rows, snap_dev = snapshots.shape
    own_rows, pairs = quad_weights.shape
    snap_parts = lax.axis_size("snaps")
    row_parts = lax.axis_size("rows")
    assert row_parts == CORES * FAR * RING and (pairs + count) % 32 == 0
    source = column_source(count)
    width = len(source)
    padded = pairs + count + -(pairs + count) % LANES
    back_source = np.zeros(pairs + count, np.int64)
    back_source[source[source >= 0]] = np.nonzero(source >= 0)[0]

    own = pl.pallas_call(
        spread_kernel,
        out_shape=jax.ShapeDtypeStruct((snap_parts, own_rows, width), jnp.bfloat16),
        scratch_shapes=[pltpu.VMEM((own_rows, padded), jnp.float32)],
    )(linear_basis, quad_weights, gather_table(source))
    maps = lax.all_to_all(own, "snaps", 0, 0, tiled=True).reshape(local_rows, width)
    coords = coordinates.reshape(FAR, RING, CORES, -1, snap_dev).transpose(2, 0, 1, 3, 4).reshape(count, snap_dev)

    block = min(BLOCK, snap_dev)
    flops = 2 * local_rows * width * snap_dev
    grad, residual = pl.pallas_call(
        lambda *refs: forward_kernel(pairs, *refs),
        out_shape=[
            jax.ShapeDtypeStruct((local_rows, width), jnp.float32),
            jax.ShapeDtypeStruct((local_rows, snap_dev), jnp.bfloat16),
        ],
        scratch_shapes=[pltpu.VMEM((width, snap_dev), jnp.bfloat16)],
        compiler_params=pltpu.CompilerParams(vmem_limit_bytes=24 << 20),
        cost_estimate=pl.CostEstimate(flops=2 * flops, bytes_accessed=4 << 20, transcendentals=0),
    )(maps, coords, snapshots)
    grad = grad.astype(jnp.float16).reshape(snap_parts, own_rows, width)
    grad_parts = lax.all_to_all(grad, "snaps", 0, 0, tiled=True)

    coord_scale = 1.0 / math.sqrt(local_rows * row_parts)
    coord_part = pl.pallas_call(
        lambda *refs: backward_kernel(coord_scale, *refs),
        grid=(snap_dev // block,),
        in_specs=[
            pl.BlockSpec((local_rows, width), lambda n: (0, 0), pipeline_mode=pl.Buffered(1)),
            pl.BlockSpec((count, block), lambda n: (0, n)),
            pl.BlockSpec((local_rows, block), lambda n: (0, n)),
        ],
        out_specs=pl.BlockSpec((count, block), lambda n: (0, n)),
        out_shape=jax.ShapeDtypeStruct((count, snap_dev), jnp.float32),
        scratch_shapes=[pltpu.VMEM((width, local_rows), jnp.bfloat16)],
        compiler_params=pltpu.CompilerParams(vmem_limit_bytes=24 << 20),
        cost_estimate=pl.CostEstimate(flops=flops, bytes_accessed=2 << 20, transcendentals=0),
    )(maps, coords, residual)

    place = lax.axis_index("rows")
    half = count // CORES
    core = place % CORES
    sent = lax.dynamic_slice_in_dim(coord_part, (1 - core) * half, half, 0)
    kept = lax.dynamic_slice_in_dim(coord_part, core * half, half, 0)
    came = lax.ppermute(sent, "rows", [(i, i ^ 1) for i in range(row_parts)])
    chips = [list(range(first, row_parts, CORES)) for first in range(CORES)]
    packed = pl.pallas_call(
        pack_kernel,
        out_shape=jax.ShapeDtypeStruct((half, snap_dev + LANES), jnp.float32),
        compiler_params=pltpu.CompilerParams(vmem_limit_bytes=4 << 20),
    )(kept, came)
    packed = packed.astype(jnp.float16).reshape(FAR * RING, -1, snap_dev + LANES)
    coord_parts = lax.all_to_all(packed, "rows", 0, 0, axis_index_groups=chips, tiled=True)
    grad_coords = pl.pallas_call(
        unpack_kernel,
        out_shape=jax.ShapeDtypeStruct((coord_parts.shape[1], snap_dev), jnp.float32),
        compiler_params=pltpu.CompilerParams(vmem_limit_bytes=4 << 20),
    )(coord_parts.astype(jnp.float32))

    model_scale = 1.0 / math.sqrt(snap_dev * snap_parts)
    grad_basis, grad_quad = pl.pallas_call(
        lambda *refs: gather_kernel(model_scale, *refs),
        out_shape=[
            jax.ShapeDtypeStruct(linear_basis.shape, jnp.float32),
            jax.ShapeDtypeStruct(quad_weights.shape, jnp.float32),
        ],
        scratch_shapes=[pltpu.VMEM((own_rows, padded), jnp.float32)],
    )(grad_parts.astype(jnp.float32), gather_table(back_source))
    return (grad_basis, grad_quad, grad_coords)


def solution(mesh):
    placed = (
        P("rows", "snaps"),
        P(("rows", "snaps"), None),
        P(("rows", "snaps"), None),
        P(None, "snaps"),
    )

    return jax.shard_map(
        shards,
        mesh=mesh,
        in_specs=placed,
        out_specs=(P(("rows", "snaps"), None), P(("rows", "snaps"), None), P("rows", "snaps")),
        check_vma=False,
    )
```

```python
import math

import jax
import jax.numpy as jnp
import numpy as np
from jax import lax
from jax.experimental import pallas as pl
from jax.experimental.pallas import tpu as pltpu
from jax.sharding import PartitionSpec as P


LANES = 128
BLOCK = 256
WIDE = 512
TOP = 14.0
CORES, FAR, RING = 2, 2, 8


def coordinate_order(count):
    each = count // (CORES * FAR * RING)
    return np.arange(count).reshape(FAR, RING, CORES, each).transpose(2, 0, 1, 3).reshape(-1)


def column_source(count):
    order = coordinate_order(count)
    offset = np.cumsum([0] + [count - i for i in range(count)])
    source = []
    for d in range(count // 2 + 1):
        for k in range(count):
            i, j = sorted((order[k], order[(k + d) % count]))
            source.append(-1 if d == count // 2 and k >= d else offset[i] + j - i)
    return np.concatenate([source, offset[-1] + order])


def gather_table(source):
    return jnp.asarray(np.concatenate([source, np.full(-len(source) % LANES, -1)]).reshape(-1, LANES).astype(np.int32))


def permuted(tiles, table_ref, row):
    source = jnp.broadcast_to(table_ref[row : row + 1], tiles[0].shape)
    lane, tile = source & (LANES - 1), source >> 7
    total = jnp.zeros(tiles[0].shape, jnp.float32)
    for number, values in enumerate(tiles):
        total = jnp.where(tile == number, jnp.take_along_axis(values, lane, axis=1), total)
    return total


def tiles_of(values):
    return [values[:, t : t + LANES] for t in range(0, values.shape[1], LANES)]


def spread_kernel(lin_ref, quad_ref, table_ref, out_ref, wide_ref):
    pairs = quad_ref.shape[1]
    wide_ref[...] = jnp.zeros_like(wide_ref)
    wide_ref[:, :pairs] = quad_ref[...].astype(jnp.float32)
    wide_ref[:, pairs : pairs + lin_ref.shape[1]] = lin_ref[...].astype(jnp.float32)
    tiles = tiles_of(wide_ref[...])
    for t in range(table_ref.shape[0]):
        moved = permuted(tiles, table_ref, t).astype(jnp.bfloat16)
        for c in range(out_ref.shape[0]):
            out_ref[c, :, t * LANES : (t + 1) * LANES] = moved


def turned(values, count, step):
    step %= count
    return values if step == 0 else jnp.concatenate([values[step:], values[:step]], axis=0)


def forward_kernel(pairs, maps_ref, coord_ref, snap_ref, grad_ref, res_ref, feat_ref):
    count, columns = coord_ref.shape
    rows, width = maps_ref.shape
    blocks = [slice(n, n + WIDE) for n in range(0, columns, WIDE)]

    def features(block):
        for start in range(block.start, block.stop, LANES):
            part = slice(start, start + LANES)
            coord = coord_ref[:, part].astype(jnp.float32)
            for r in range(8):
                shifted = coord if r == 0 else pltpu.roll(coord, count - r, 0)
                for d in range(r, count // 2 + 1, 8):
                    feat_ref[d * count : (d + 1) * count, part] = (
                        coord * turned(shifted, count, d - r)
                    ).astype(jnp.bfloat16)
            feat_ref[width - count :, part] = coord_ref[:, part]

    features(blocks[0])
    for n, block in enumerate(blocks):
        rebuilt = jnp.dot(maps_ref[...], feat_ref[:, block], preferred_element_type=jnp.float32)
        if n + 1 < len(blocks):
            features(blocks[n + 1])
        res_ref[:, block] = (rebuilt - snap_ref[:, block].astype(jnp.float32)).astype(jnp.bfloat16)
    top = jnp.zeros((rows, LANES), jnp.float32)
    for start in range(0, width, WIDE):
        part = slice(start, min(start + WIDE, width))
        grad = lax.dot_general(
            res_ref[...], feat_ref[part], (((1,), (1,)), ((), ())), preferred_element_type=jnp.float32
        )
        grad_ref[:, part] = grad
        for tile in tiles_of(grad):
            top = jnp.maximum(top, jnp.abs(tile))
    top = jnp.max(jnp.max(top, axis=0, keepdims=True), axis=1, keepdims=True)
    level = jnp.floor(jnp.log2(jnp.maximum(top, 2.0**-100)))
    scale = jnp.exp2(TOP - level)
    for start in range(0, width, LANES):
        part = slice(start, start + LANES)
        values = grad_ref[:, part] * scale
        if start <= pairs < start + LANES:
            lane = lax.broadcasted_iota(jnp.int32, values.shape, 1) + start
            values = jnp.where((lane >= pairs) & (lane < width - count), level, values)
        grad_ref[:, part] = values


def backward_kernel(scale, maps_ref, coord_ref, res_ref, out_ref, turn_ref):
    count = coord_ref.shape[0]
    width = maps_ref.shape[1]

    @pl.when(pl.program_id(0) == 0)
    def _():
        turn_ref[...] = maps_ref[...].astype(jnp.float32).T.astype(jnp.bfloat16)

    coord = coord_ref[...].astype(jnp.float32)
    residual = res_ref[...]

    def back(row):
        return jnp.dot(turn_ref[row : row + count], residual, preferred_element_type=jnp.float32)

    total = back(width - count)
    for r in range(8):
        shifted = coord if r == 0 else pltpu.roll(coord, count - r, 0)
        spun = jnp.zeros_like(coord)
        for d in range(r, count // 2 + 1, 8):
            part = back(d * count)
            total = total + part * turned(shifted, count, d - r)
            spun = spun + turned(part * coord, count, r - d)
        total = total + (spun if r == 0 else pltpu.roll(spun, r, 0))
    out_ref[...] = total * scale


def pack_kernel(kept_ref, came_ref, out_ref):
    columns = kept_ref.shape[1]
    total = kept_ref[...] + came_ref[...]
    top = jnp.max(jnp.max(jnp.abs(total), axis=0, keepdims=True), axis=1, keepdims=True)
    level = jnp.floor(jnp.log2(jnp.maximum(top, 2.0**-100)))
    out_ref[:, :columns] = total * jnp.exp2(TOP - level)
    out_ref[:, columns:] = jnp.broadcast_to(level, (total.shape[0], LANES))


def unpack_kernel(parts_ref, out_ref):
    columns = out_ref.shape[1]
    total = jnp.zeros(out_ref.shape, jnp.float32)
    for p in range(parts_ref.shape[0]):
        part = parts_ref[p]
        total = total + part[:, :columns] * jnp.exp2(part[:, columns : columns + 1] - TOP)
    out_ref[...] = total


def gather_kernel(scale, parts_ref, table_ref, lin_ref, quad_ref, wide_ref):
    pairs = quad_ref.shape[1]
    total = jnp.zeros(parts_ref.shape[1:], jnp.float32)
    for p in range(parts_ref.shape[0]):
        part = parts_ref[p]
        total = total + part * jnp.exp2(part[:, pairs : pairs + 1] - TOP)
    tiles = tiles_of(total * scale)
    for t in range(table_ref.shape[0]):
        wide_ref[:, t * LANES : (t + 1) * LANES] = permuted(tiles, table_ref, t)
    quad_ref[...] = wide_ref[:, :pairs]
    lin_ref[...] = wide_ref[:, pairs : pairs + lin_ref.shape[1]]


def shards(snapshots, linear_basis, quad_weights, coordinates):
    count = coordinates.shape[0]
    local_rows, snap_dev = snapshots.shape
    own_rows, pairs = quad_weights.shape
    snap_parts = lax.axis_size("snaps")
    row_parts = lax.axis_size("rows")
    assert row_parts == CORES * FAR * RING and (pairs + count) % 32 == 0
    source = column_source(count)
    width = len(source)
    padded = pairs + count + -(pairs + count) % LANES
    back_source = np.zeros(pairs + count, np.int64)
    back_source[source[source >= 0]] = np.nonzero(source >= 0)[0]

    own = pl.pallas_call(
        spread_kernel,
        out_shape=jax.ShapeDtypeStruct((snap_parts, own_rows, width), jnp.bfloat16),
        scratch_shapes=[pltpu.VMEM((own_rows, padded), jnp.float32)],
    )(linear_basis, quad_weights, gather_table(source))
    place = lax.axis_index("rows")
    core = place % CORES
    both = ("rows", "snaps")
    spread = [int(f"{z:04b}"[::-1], 2) for z in range(snap_parts)]
    lines = [[r * snap_parts + z for z in spread][:: 1 - 2 * (r % CORES)] for r in range(row_parts)]
    maps = lax.all_to_all(own, both, 0, 0, axis_index_groups=lines, tiled=True).reshape(local_rows, width)
    stacked = snapshots.reshape(2, 2, 2, 2, own_rows, snap_dev).transpose(3, 2, 1, 0, 4, 5)
    stacked = stacked.reshape(snap_parts, own_rows, snap_dev)
    snapshots = jnp.where(core == 1, stacked[::-1], stacked).reshape(local_rows, snap_dev)
    coords = coordinates.reshape(FAR, RING, CORES, -1, snap_dev).transpose(2, 0, 1, 3, 4).reshape(count, snap_dev)

    block = min(BLOCK, snap_dev)
    flops = 2 * local_rows * width * snap_dev
    grad, residual = pl.pallas_call(
        lambda *refs: forward_kernel(pairs, *refs),
        out_shape=[
            jax.ShapeDtypeStruct((local_rows, width), jnp.float32),
            jax.ShapeDtypeStruct((local_rows, snap_dev), jnp.bfloat16),
        ],
        scratch_shapes=[pltpu.VMEM((width, snap_dev), jnp.bfloat16)],
        compiler_params=pltpu.CompilerParams(vmem_limit_bytes=24 << 20),
        cost_estimate=pl.CostEstimate(flops=2 * flops, bytes_accessed=4 << 20, transcendentals=0),
    )(maps, coords, snapshots)
    grad = grad.astype(jnp.float16).reshape(snap_parts, own_rows, width)
    grad_parts = lax.all_to_all(grad, both, 0, 0, axis_index_groups=lines, tiled=True)

    coord_scale = 1.0 / math.sqrt(local_rows * row_parts)
    coord_part = pl.pallas_call(
        lambda *refs: backward_kernel(coord_scale, *refs),
        grid=(snap_dev // block,),
        in_specs=[
            pl.BlockSpec((local_rows, width), lambda n: (0, 0), pipeline_mode=pl.Buffered(1)),
            pl.BlockSpec((count, block), lambda n: (0, n)),
            pl.BlockSpec((local_rows, block), lambda n: (0, n)),
        ],
        out_specs=pl.BlockSpec((count, block), lambda n: (0, n)),
        out_shape=jax.ShapeDtypeStruct((count, snap_dev), jnp.float32),
        scratch_shapes=[pltpu.VMEM((width, local_rows), jnp.bfloat16)],
        compiler_params=pltpu.CompilerParams(vmem_limit_bytes=24 << 20),
        cost_estimate=pl.CostEstimate(flops=flops, bytes_accessed=2 << 20, transcendentals=0),
    )(maps, coords, residual)

    half = count // CORES
    sent = lax.dynamic_slice_in_dim(coord_part, (1 - core) * half, half, 0)
    kept = lax.dynamic_slice_in_dim(coord_part, core * half, half, 0)
    came = lax.ppermute(sent, "rows", [(i, i ^ 1) for i in range(row_parts)])
    chips = [list(range(first, row_parts, CORES))[:: 1 - 2 * first] for first in range(CORES)]
    packed = pl.pallas_call(
        pack_kernel,
        out_shape=jax.ShapeDtypeStruct((half, snap_dev + LANES), jnp.float32),
        compiler_params=pltpu.CompilerParams(vmem_limit_bytes=4 << 20),
    )(kept, came)
    packed = packed.astype(jnp.float16).reshape(FAR * RING, -1, snap_dev + LANES)
    packed = jnp.where(core == 1, packed[::-1], packed)
    coord_parts = lax.all_to_all(packed, "rows", 0, 0, axis_index_groups=chips, tiled=True)
    grad_coords = pl.pallas_call(
        unpack_kernel,
        out_shape=jax.ShapeDtypeStruct((coord_parts.shape[1], snap_dev), jnp.float32),
        compiler_params=pltpu.CompilerParams(vmem_limit_bytes=4 << 20),
    )(coord_parts.astype(jnp.float32))

    model_scale = 1.0 / math.sqrt(snap_dev * snap_parts)
    grad_basis, grad_quad = pl.pallas_call(
        lambda *refs: gather_kernel(model_scale, *refs),
        out_shape=[
            jax.ShapeDtypeStruct(linear_basis.shape, jnp.float32),
            jax.ShapeDtypeStruct(quad_weights.shape, jnp.float32),
        ],
        scratch_shapes=[pltpu.VMEM((own_rows, padded), jnp.float32)],
    )(grad_parts.astype(jnp.float32), gather_table(back_source))
    return (grad_basis, grad_quad, grad_coords)


def solution(mesh):
    placed = (
        P("rows", "snaps"),
        P(("rows", "snaps"), None),
        P(("rows", "snaps"), None),
        P(None, "snaps"),
    )

    return jax.shard_map(
        shards,
        mesh=mesh,
        in_specs=placed,
        out_specs=(P(("rows", "snaps"), None), P(("rows", "snaps"), None), P("rows", "snaps")),
        check_vma=False,
    )
```
